512 devices in a mesh: ctx: 64 (over z_lo, y, core), grp: 8 (over x, z_hi).
Axes of the slice: x: 4, y: 4, z: 16 (z_hi: 2, z_lo: 8; z = z_hi * 8 + z_lo), core: 2. Of those that a mesh axis runs over, the one named last changes fastest.
Arguments:
- queries: bfloat16 [8192, 4096], P('ctx', 'grp'), may hold values from -6 to 6
- keys: bfloat16 [8192, 4096], P('ctx', 'grp'), may hold values from -6 to 6
- values: bfloat16 [8192, 4096], P('ctx', 'grp'), may hold values from -6 to 6
- block_order: int32 [128], replicated, may hold values from 0 to 127, each once
- token_ids: int32 [8192], P('ctx'), may hold values from 0 to 511
- stream_table: bfloat16 [4, 512, 8192], P(None, None, 'grp'), may hold values from -70 to 70
- short_filter: float32 [3, 7, 8192], P(None, None, 'grp'), may hold values from -2 to 2
- long_filter: bfloat16 [512, 128], P('grp'), may hold values from -0.5 to 0.5
- norm_gain: float32 [8192], P('grp'), may hold values from 0.1 to 1.9
Outputs:
- attended: bfloat16 [8192, 4096], P('ctx', 'grp')
- hyena_out: bfloat16 [8192, 8192], P('ctx', 'grp')
The draws below stay inside these ranges and needn't reach their ends.
All inputs are finite; a program needn't handle non-finite values.
Results may differ from the reference program's by a relative error of at most 0.004.
Values may be sent and summed in bfloat16 or wider, within the bound.
No kernel may reach another device: no remote copies, remote signals or barrier semaphores. Data moves between devices by JAX's collectives and lax.ppermute only.
A program may use at most 128 MiB of HBM per device.

```python
import math
import jax
import jax.numpy as jnp
from jax import lax

HD = 128
HEADS = 32
CHANNELS = 8192
GSIZE = 16
FILTERS = 512
TAPS = 128
SHORT = 7
VOCAB = 512
TOK_DEV = 128
SEQ = 8192
N_CTX = 64


def base_draw(key, salt):
    inner = jax.random.fold_in(key, salt)
    return jnp.clip(1.6 * jax.random.normal(inner, (SEQ, HEADS * HD), jnp.float32), -6.0, 6.0)


def draw_queries(key, part):
    result = base_draw(key, 11)
    return result.astype(jnp.bfloat16)


def draw_keys(key, part):
    result = base_draw(key, 12)
    return result.astype(jnp.bfloat16)


def draw_stream_table(key, part):
    picks = jax.random.split(jax.random.fold_in(key, 907), 2)
    column = jnp.arange(CHANNELS, dtype=jnp.float32) / CHANNELS
    row_level = jax.random.uniform(picks[1], (1, VOCAB, 1), jnp.float32)
    result = jnp.clip(jax.random.normal(picks[0], (4, VOCAB, CHANNELS), jnp.float32), -4.0, 4.0)
    ramp = 0.2 * 10.0 ** column
    scaled = result * ramp[None, None, :] * 10.0 ** (row_level - 0.5)
    stream = jnp.arange(4)[:, None, None]
    return jnp.where(stream == 0, scaled, result).astype(jnp.bfloat16)


def touch_ends(array, rng, smallest, high):
    longest = array.shape.index(max(array.shape))
    spots = []
    for shift in (0, 1):
        where = [jax.random.randint(jax.random.fold_in(rng, axis), (), 0, length) for axis, length in enumerate(array.shape)]
        where[longest] = (where[longest] + shift) % array.shape[longest]
        spots.append(tuple(where))
    return array.at[spots[0]].set(smallest).at[spots[1]].set(high)


def levels(key, extent, pieces, smallest, top_value):
    factor_of = 1.0
    for axis_at, shards_of in pieces:
        steps = jax.random.uniform(jax.random.fold_in(jax.random.fold_in(key, 6), axis_at), (shards_of,), jnp.float32, smallest / len(pieces), top_value / len(pieces))
        factor_of = factor_of * jnp.repeat(jnp.exp(steps), extent[axis_at] // shards_of).reshape((-1,) + (1,) * (len(extent) - 1 - axis_at))
    return factor_of


def scatter_about(own_key, extent, width, reach, shards=(), kind=jnp.bfloat16):
    drawn = jax.random.normal(own_key, extent, jnp.float32) * width
    if len(shards) > 0:
        drawn = levels(own_key, extent, shards, -0.22, 0.18) * drawn
    return jnp.clip(drawn, min=-reach, max=reach).astype(kind)


def setup_inputs(seed: int = 0) -> dict:
    streams_of = jax.random.split(jax.random.key(seed), 10)
    queries = draw_queries(jax.random.fold_in(streams_of[9], 71), 0)
    keys = draw_keys(jax.random.fold_in(streams_of[9], 71), 0)
    values = scatter_about(streams_of[2], (SEQ, HEADS * HD), 1.0, 6.0, ((0, 64), (1, 8)))
    block_order = jax.random.permutation(streams_of[3], 2 * N_CTX).astype(jnp.int32)
    token_ids = touch_ends(jax.random.randint(streams_of[4], (SEQ,), 0, VOCAB), jax.random.fold_in(streams_of[4], 1), 0, VOCAB - 1).astype(jnp.int32)
    stream_table = draw_stream_table(jax.random.fold_in(streams_of[9], 71), 0)
    short_filter = scatter_about(streams_of[6], (3, SHORT, CHANNELS), SHORT ** -0.5, 2.0, ((2, 8),), jnp.float32)
    long_filter = scatter_about(streams_of[7], (FILTERS, TAPS), TAPS ** -0.5, 0.5, ((0, 8),))
    norm_gain = jnp.clip(1.0 + 0.18 * jax.random.normal(streams_of[8], (CHANNELS,), jnp.float32), 0.1, 1.9)
    return dict(queries=queries, keys=keys, values=values, block_order=block_order, token_ids=token_ids, stream_table=stream_table, short_filter=short_filter, long_filter=long_filter, norm_gain=norm_gain)


def reference(queries, keys, values, block_order, token_ids, stream_table, short_filter, long_filter, norm_gain):
    seq_len = queries.shape[0]
    half_rows = TOK_DEV // 2
    row_index = jnp.arange(seq_len, dtype=jnp.int32)
    slot = (2 * (row_index // TOK_DEV) + row_index % TOK_DEV // half_rows).astype(jnp.int32)
    position = block_order[slot] * half_rows + row_index % half_rows
    score_scale = 1.0 / math.sqrt(HD)
    block_rows = math.gcd(seq_len, 1024)
    query_heads = queries.reshape(seq_len, HEADS, HD).transpose(1, 0, 2)
    key_heads = keys.reshape(seq_len, HEADS, HD).transpose(1, 0, 2)
    value_heads = values.reshape(seq_len, HEADS, HD).transpose(1, 0, 2)

    def one_head(operands):
        head_q, head_k, head_v = operands

        def one_block(offset):
            block_q = lax.dynamic_slice_in_dim(head_q, offset, block_rows, 0)
            block_pos = lax.dynamic_slice_in_dim(position, offset, block_rows, 0)
            scores = jnp.dot(block_q, head_k.T, preferred_element_type=jnp.float32) * score_scale
            visible = position[None, :] <= block_pos[:, None]
            scores = jnp.where(visible, scores, -1e+30)
            row_peak = lax.optimization_barrier(jnp.max(scores, axis=1, keepdims=True))
            weights = jnp.where(visible, jnp.exp(scores - row_peak), 0.0)
            row_total = lax.optimization_barrier(jnp.sum(weights, axis=1, keepdims=True))
            summed = jnp.dot(weights.astype(jnp.bfloat16), head_v, preferred_element_type=jnp.float32)
            return (summed / row_total).astype(jnp.bfloat16)
        offsets = (jnp.arange(seq_len // block_rows) * block_rows).astype(jnp.int32)
        return lax.map(one_block, offsets).reshape(seq_len, HD)
    attended = lax.map(one_head, (query_heads, key_heads, value_heads))
    attended = attended.transpose(1, 0, 2).reshape(seq_len, HEADS * HD)
    feats = stream_table[:, token_ids, :]
    shorts = []
    for stream in range(3):
        source = feats[stream + 1].astype(jnp.float32)
        padded = jnp.pad(source, ((SHORT - 1, 0), (0, 0)))
        running = jnp.zeros((seq_len, CHANNELS), jnp.float32)
        for lag_step in range(SHORT):
            running = running + short_filter[stream, lag_step][None, :] * padded[SHORT - 1 - lag_step:SHORT - 1 - lag_step + seq_len]
        shorts.append(running)
    product = (shorts[0] * shorts[2]).astype(jnp.bfloat16)
    spread = jnp.repeat(long_filter.astype(jnp.float32), GSIZE, axis=0).T
    product_pad = jnp.pad(product.astype(jnp.float32), ((TAPS - 1, 0), (0, 0)))

    def add_tap(tap_index, running):
        window = lax.dynamic_slice_in_dim(product_pad, TAPS - 1 - tap_index, seq_len, 0)
        tap_row = lax.dynamic_slice_in_dim(spread, tap_index, 1, 0)
        return running + tap_row * window
    convolved = lax.fori_loop(0, TAPS, add_tap, jnp.zeros((seq_len, CHANNELS), jnp.float32))
    mixed = feats[0].astype(jnp.float32) + shorts[1] * convolved
    mean_square = lax.optimization_barrier(jnp.mean(mixed * mixed, axis=1, keepdims=True))
    hyena_out = (mixed * norm_gain[None, :] / jnp.sqrt(mean_square + 1e-06)).astype(jnp.bfloat16)
    return (attended, hyena_out)
```

```python
import math

import jax
import jax.numpy as jnp
from jax import lax
from jax.experimental import pallas as pl
from jax.experimental.pallas import tpu as pltpu
from jax.sharding import Mesh, PartitionSpec as P

HD = 128
ROWS = 128
HALF = 64
QUADS = 4
YS = 4
SHORT = 7
TAPS = 128
GSIZE = 16
CHAN_BLOCK = 256
STAT_ROWS = 16

neg_fill = -1e30
eps_norm = 1e-06

f32 = jnp.float32
bf16 = jnp.bfloat16
CTX = ("zq", "zp", "y", "c")


def vmem_spec():
    return pl.BlockSpec(memory_space=pltpu.VMEM)


def smem_spec():
    return pl.BlockSpec(memory_space=pltpu.SMEM)


def params(**kw):
    return pltpu.CompilerParams(vmem_limit_bytes=48 * 1024 * 1024, **kw)


def pack_kernel(q_hbm, k_hbm, v_hbm, out_ref, buf, sems):
    copies = []
    for n, ref in enumerate((q_hbm, k_hbm, v_hbm)):
        copies.append(pltpu.make_async_copy(ref, buf.at[n], sems.at[n]))
        copies[-1].start()
    for n, copy in enumerate(copies):
        copy.wait()
        for head in range(QUADS):
            out_ref[head, n * ROWS : (n + 1) * ROWS] = buf[n, :, head * HD : (head + 1) * HD]


def pack(queries, keys, values):
    return pl.pallas_call(
        pack_kernel,
        out_shape=jax.ShapeDtypeStruct((QUADS, 3 * ROWS, HD), bf16),
        in_specs=[pl.BlockSpec(memory_space=pl.ANY)] * 3,
        out_specs=vmem_spec(),
        scratch_shapes=[
            pltpu.VMEM((3,) + queries.shape, bf16),
            pltpu.SemaphoreType.DMA((3,)),
        ],
        compiler_params=pltpu.CompilerParams(vmem_limit_bytes=60 * 1024 * 1024),
        cost_estimate=pl.CostEstimate(flops=0, bytes_accessed=786432, transcendentals=0),
        name="pack",
    )(queries, keys, values)


TILE = QUADS * ROWS


def attend_kernel(where_ref, order_ref, *refs):
    q_ref, kv_refs = refs[0], refs[1:5]
    out_ref, k_all, vt_all, scores, key_pos = refs[5:]
    zp, y, c = where_ref[0], where_ref[1], where_ref[2]
    scale2 = math.log2(math.e) / math.sqrt(HD)
    for n in range(4):
        low = ROWS if n == 0 else 0
        k_all[n] = kv_refs[n][:, low : low + ROWS].reshape(TILE, HD)
        vt_all[n] = kv_refs[n][:, low + ROWS : low + 2 * ROWS].reshape(TILE, HD).T
        kz = zp ^ (n & 1)
        kc = c ^ (n >> 1)
        for quad in range(QUADS):
            dev = quad * 16 + kz * 8 + y * 2 + kc
            for half in range(2):
                start = order_ref[2 * dev + half] * HALF
                key_pos[n, pl.ds((quad * 2 + half) * HALF, HALF), :] = (
                    lax.broadcasted_iota(jnp.int32, (HALF, 128), 0) + start
                )

    lane = lax.broadcasted_iota(jnp.int32, (1, 128), 1)

    def one_block(qy, carry):
        pieces = []
        for quad in range(QUADS):
            dev = quad * 16 + zp * 8 + qy * 2 + c
            first = order_ref[2 * dev] * HALF
            second = order_ref[2 * dev + 1] * HALF - HALF
            pieces.append(lane + jnp.where(lane < HALF, first, second))
        q_blk = q_ref[qy].reshape(TILE, HD)
        peak = jnp.full((1, TILE), neg_fill, f32)
        for n in range(4):
            s = lax.dot_general(
                k_all[n], q_blk, (((1,), (1,)), ((), ())), preferred_element_type=f32
            )
            kp = key_pos[n]
            cols = []
            for quad in range(QUADS):
                visible = kp <= pieces[quad]
                cols.append(jnp.where(visible, s[:, quad * 128 : (quad + 1) * 128], neg_fill))
            s = jnp.concatenate(cols, axis=1)
            scores[n] = s
            peak = jnp.maximum(peak, jnp.max(s, axis=0, keepdims=True))
        total = jnp.zeros((1, TILE), f32)
        acc = jnp.zeros((HD, TILE), f32)
        for n in range(4):
            p = jnp.exp2((scores[n] - peak) * scale2)
            total = total + jnp.sum(p, axis=0, keepdims=True)
            acc = acc + jnp.dot(vt_all[n], p.astype(bf16), preferred_element_type=f32)
        out_ref[qy, 0:HD, :] = acc.astype(bf16)
        rows = []
        for stat in (peak, total):
            rest = stat
            for piece in range(3):
                part = rest.astype(bf16).astype(f32)
                rows.append(part)
                rest = rest - part
        rows.append(jnp.zeros((STAT_ROWS - 6, TILE), f32))
        out_ref[qy, HD : HD + STAT_ROWS, :] = jnp.concatenate(rows, axis=0).astype(bf16)
        return carry

    lax.fori_loop(0, 4, one_block, 0)


def attend(where, order, q_all, kv_blocks):
    return pl.pallas_call(
        attend_kernel,
        out_shape=jax.ShapeDtypeStruct((YS, HD + STAT_ROWS, TILE), bf16),
        in_specs=[smem_spec(), smem_spec()] + [vmem_spec()] * 5,
        out_specs=vmem_spec(),
        scratch_shapes=[
            pltpu.VMEM((4, TILE, HD), bf16),
            pltpu.VMEM((4, HD, TILE), bf16),
            pltpu.VMEM((4, TILE, TILE), f32),
            pltpu.VMEM((4, TILE, 128), jnp.int32),
        ],
        compiler_params=params(),
        cost_estimate=pl.CostEstimate(
            flops=4 * 2048 * 2048 * 128, bytes_accessed=2 << 20, transcendentals=1 << 22
        ),
        name="attend",
    )(where, order, q_all, *kv_blocks)


def merge_kernel(part_ref, out_ref):
    scale2 = math.log2(math.e) / math.sqrt(HD)
    peaks, totals = [], []
    for n in range(YS):
        stats = part_ref[n, HD : HD + STAT_ROWS, :].astype(f32)
        peaks.append((stats[0:1] + stats[1:2]) + stats[2:3])
        totals.append((stats[3:4] + stats[4:5]) + stats[5:6])
    peak = jnp.maximum(jnp.maximum(peaks[0], peaks[1]), jnp.maximum(peaks[2], peaks[3]))
    factors = [jnp.exp2((one - peak) * scale2) for one in peaks]
    total = sum(f * t for f, t in zip(factors, totals))
    inverse = 1.0 / total
    acc = jnp.zeros((HD, TILE), f32)
    for n in range(YS):
        acc = acc + part_ref[n, 0:HD, :].astype(f32) * (factors[n] * inverse)
    for quad in range(QUADS):
        out_ref[quad] = acc[:, quad * ROWS : (quad + 1) * ROWS].T.astype(bf16)


def merge(parts):
    return pl.pallas_call(
        merge_kernel,
        out_shape=jax.ShapeDtypeStruct((QUADS, ROWS, HD), bf16),
        in_specs=[vmem_spec()],
        out_specs=vmem_spec(),
        compiler_params=params(),
        cost_estimate=pl.CostEstimate(flops=1 << 20, bytes_accessed=720896, transcendentals=4096),
        name="merge",
    )(parts)


def unpack_kernel(x_ref, out_ref):
    for head in range(QUADS):
        out_ref[:, head * HD : (head + 1) * HD] = x_ref[head]


def unpack(blocks):
    return pl.pallas_call(
        unpack_kernel,
        out_shape=jax.ShapeDtypeStruct((ROWS, QUADS * HD), bf16),
        in_specs=[vmem_spec()],
        out_specs=vmem_spec(),
        compiler_params=params(),
        cost_estimate=pl.CostEstimate(flops=0, bytes_accessed=262144, transcendentals=0),
        name="unpack",
    )(blocks)


EXT = 16 + 2 * ROWS


def hyena_kernel(
    rank_ref, far_ref, near_ref, own_ref, table_ref, short_ref, long_ref,
    mixed_ref, squares_ref, hot, feats_a, feats_b, prod, base, sq,
):
    step = pl.program_id(0)
    rank = rank_ref[0]
    vocab = table_ref.shape[1]

    @pl.when(step == 0)
    def _():
        lane = lax.broadcasted_iota(jnp.int32, (128, 128), 1)

        def column(ref, valid):
            ids = jnp.where(valid, ref[...], -1)
            return jnp.broadcast_to(ids, (128, 128)).T

        for ref, valid, low, at, count in (
            (far_ref, rank >= 2, 112, 0, 16),
            (near_ref, rank >= 1, 0, 16, 128),
            (own_ref, rank >= 0, 0, 144, 128),
        ):
            col = column(ref, valid)[low : low + count]
            for v in range(vocab // 128):
                hit = col == lane[low : low + count] + v * 128
                hot[at : at + count, v * 128 : (v + 1) * 128] = jnp.where(hit, 1.0, 0.0).astype(bf16)
        sq[...] = jnp.zeros_like(sq)
        tap = lax.broadcasted_iota(jnp.int32, (TAPS, 2 * ROWS), 0)
        spot = lax.broadcasted_iota(jnp.int32, (TAPS, 2 * ROWS), 1)
        flip = jnp.where(tap + spot == TAPS, 1.0, 0.0).astype(bf16)
        base[...] = jnp.dot(long_ref[...], flip, preferred_element_type=f32)

    feats_a[...] = jnp.dot(hot[...], table_ref[1], preferred_element_type=f32)
    feats_b[...] = jnp.dot(hot[...], table_ref[3], preferred_element_type=f32)

    def short_mix(ref, stream, low, count, lanes):
        running = jnp.zeros((count, 128), f32)
        for k in range(SHORT):
            running = running + short_ref[stream, k : k + 1, lanes] * ref[low - k : low - k + count, lanes]
        return running

    for lb in range(CHAN_BLOCK // 128):
        lanes = slice(lb * 128, (lb + 1) * 128)
        for low in (16, 144):
            one = short_mix(feats_a, 0, low, 128, lanes)
            three = short_mix(feats_b, 2, low, 128, lanes)
            prod[low - 16 : low + 112, lanes] = (one * three).astype(bf16)
    feats_a[128:, :] = jnp.dot(hot[128:, :], table_ref[2], preferred_element_type=f32)
    feats_b[144:, :] = jnp.dot(hot[144:, :], table_ref[0], preferred_element_type=f32)
    chan = lax.broadcasted_iota(jnp.int32, (ROWS, CHAN_BLOCK), 1) // GSIZE
    groups_here = CHAN_BLOCK // GSIZE
    window = base[pl.ds(pl.multiple_of(step * groups_here, groups_here), groups_here)]
    conv = jnp.zeros((ROWS, CHAN_BLOCK), f32)
    for g in range(groups_here):
        row = jnp.broadcast_to(window[g : g + 1], (ROWS, 2 * ROWS))
        lags = pltpu.roll(row, 0, 1, stride=1, stride_axis=0).astype(bf16)
        every = jnp.dot(lags, prod[...], preferred_element_type=f32)
        conv = jnp.where(chan == g, every, conv)
    for lb in range(CHAN_BLOCK // 128):
        lanes = slice(lb * 128, (lb + 1) * 128)
        acc = conv[:, lanes]
        two = short_mix(feats_a, 1, 144, ROWS, lanes)
        mixed = feats_b[144:, lanes] + two * acc
        mixed_ref[:, lanes] = mixed
        sq[...] += mixed * mixed

    @pl.when(step == pl.num_programs(0) - 1)
    def _():
        squares_ref[...] = jnp.sum(sq[...].T, axis=0, keepdims=True)


def hyena(rank, far, near, own, table, short_filter, long_filter):
    streams, vocab, channels = table.shape
    return pl.pallas_call(
        hyena_kernel,
        grid=(channels // CHAN_BLOCK,),
        out_shape=(
            jax.ShapeDtypeStruct((ROWS, channels), f32),
            jax.ShapeDtypeStruct((1, ROWS), f32),
        ),
        in_specs=[
            smem_spec(),
            pl.BlockSpec((1, ROWS), lambda i: (0, 0)),
            pl.BlockSpec((1, ROWS), lambda i: (0, 0)),
            pl.BlockSpec((1, ROWS), lambda i: (0, 0)),
            pl.BlockSpec((streams, vocab, CHAN_BLOCK), lambda i: (0, 0, i)),
            pl.BlockSpec((3, SHORT, CHAN_BLOCK), lambda i: (0, 0, i)),
            pl.BlockSpec(long_filter.shape, lambda i: (0, 0)),
        ],
        out_specs=(
            pl.BlockSpec((ROWS, CHAN_BLOCK), lambda i: (0, i)),
            pl.BlockSpec((1, ROWS), lambda i: (0, 0)),
        ),
        scratch_shapes=[
            pltpu.VMEM((EXT, vocab), bf16),
            pltpu.VMEM((EXT, CHAN_BLOCK), f32),
            pltpu.VMEM((EXT, CHAN_BLOCK), f32),
            pltpu.VMEM((2 * ROWS, CHAN_BLOCK), bf16),
            pltpu.VMEM((long_filter.shape[0], 2 * ROWS), f32),
            pltpu.VMEM((ROWS, 128), f32),
        ],
        compiler_params=pltpu.CompilerParams(
            vmem_limit_bytes=60 * 1024 * 1024, dimension_semantics=("arbitrary",)
        ),
        cost_estimate=pl.CostEstimate(flops=1 << 30, bytes_accessed=5 << 20, transcendentals=0),
        name="hyena",
    )(rank, far, near, own, table, short_filter, long_filter)


def norm_kernel(channels, mixed_ref, squares_ref, gain_ref, out_ref):
    mean = squares_ref[...] / channels
    inverse = jnp.broadcast_to(lax.rsqrt(mean + eps_norm), (ROWS, ROWS)).T
    for lb in range(mixed_ref.shape[1] // 128):
        lanes = slice(lb * 128, (lb + 1) * 128)
        out_ref[:, lanes] = (mixed_ref[:, lanes] * gain_ref[:, lanes] * inverse).astype(bf16)


def norm(mixed, squares, gain, channels):
    def kernel(*refs):
        norm_kernel(channels, *refs)

    return pl.pallas_call(
        kernel,
        out_shape=jax.ShapeDtypeStruct(mixed.shape, bf16),
        in_specs=[vmem_spec()] * 3,
        out_specs=vmem_spec(),
        compiler_params=params(),
        cost_estimate=pl.CostEstimate(flops=1 << 18, bytes_accessed=800000, transcendentals=128),
        name="norm",
    )(mixed, squares, gain)


def across(squares, stride):
    groups = lax.axis_size("g")
    if stride >= groups:
        return squares
    return squares + lax.ppermute(squares, "g", [(i ^ stride, i) for i in range(groups)])


def body(
    queries, keys, values, block_order, token_ids, stream_table, short_filter, long_filter, norm_gain
):
    groups = lax.axis_size("g")
    zp, y, c = lax.axis_index("zp"), lax.axis_index("y"), lax.axis_index("c")
    rank = ((lax.axis_index("zq") * 2 + zp) * 4 + y) * 2 + c
    devices = QUADS * 2 * YS * 2

    own = lax.all_to_all(pack(queries, keys, values), "zq", 0, 0)

    near = lax.ppermute(token_ids, CTX, [(i, i + 1) for i in range(devices - 1)])
    far = lax.ppermute(token_ids, CTX, [(i, i + 2) for i in range(devices - 2)])
    mixed, squares = hyena(
        rank.reshape(1), far[None], near[None], token_ids[None],
        stream_table, short_filter, long_filter,
    )
    squares = across(squares, 1)
    own, mixed, squares = lax.optimization_barrier((own, mixed, squares))

    q_all = lax.all_to_all(jnp.broadcast_to(own[None, :, 0:ROWS], (YS, QUADS, ROWS, HD)), "y", 0, 0)
    swap = [(0, 1), (1, 0)]
    kv_own = own[:, ROWS:]
    kv_z = lax.ppermute(kv_own, "zp", swap)
    kv_c = lax.ppermute(kv_own, "c", swap)
    kv_zc = lax.ppermute(kv_z, "c", swap)
    where = jnp.stack([zp, y, c])
    parts = attend(where, block_order, q_all, [own, kv_z, kv_c, kv_zc])
    parts, squares = lax.optimization_barrier((parts, squares))
    parts = lax.all_to_all(parts, "y", 0, 0)
    for stride in (2, 4):
        squares = across(squares, stride)
    parts, squares = lax.optimization_barrier((parts, squares))
    blocks = lax.all_to_all(merge(parts), "zq", 0, 0)
    hyena_out = norm(mixed, squares, norm_gain[None], stream_table.shape[2] * groups)
    blocks, hyena_out = lax.optimization_barrier((blocks, hyena_out))
    return (unpack(blocks), hyena_out)


def solution(mesh):
    groups = mesh.shape["grp"]
    fine = Mesh(mesh.devices.reshape(QUADS, 2, YS, 2, groups), CTX + ("g",))
    placed = (
        P(CTX, "g"),
        P(CTX, "g"),
        P(CTX, "g"),
        P(),
        P(CTX),
        P(None, None, "g"),
        P(None, None, "g"),
        P("g", None),
        P("g"),
    )
    return jax.shard_map(
        body,
        mesh=fine,
        in_specs=placed,
        out_specs=(P(CTX, "g"), P(CTX, "g")),
        check_vma=False,
    )
```

```python
import math

import jax
import jax.numpy as jnp
from jax import lax
from jax.experimental import pallas as pl
from jax.experimental.pallas import tpu as pltpu
from jax.sharding import Mesh, PartitionSpec as P


HD = 128
ROWS = 128
HALF = 64
QUADS = 4
YS = 4
SHORT = 7
TAPS = 128
GSIZE = 16
CHAN_BLOCK = 256
STAT_ROWS = 16

neg_fill = -1e30
eps_norm = 1e-06

f32 = jnp.float32
bf16 = jnp.bfloat16
CTX = ("zp", "zq", "y", "c")


def vmem_spec():
    return pl.BlockSpec(memory_space=pltpu.VMEM)


def smem_spec():
    return pl.BlockSpec(memory_space=pltpu.SMEM)


def params(**kw):
    return pltpu.CompilerParams(vmem_limit_bytes=48 * 1024 * 1024, **kw)


def pack_kernel(q_hbm, k_hbm, v_hbm, out_ref, buf, sems):
    copies = []
    for n, ref in enumerate((q_hbm, k_hbm, v_hbm)):
        copies.append(pltpu.make_async_copy(ref, buf.at[n], sems.at[n]))
        copies[-1].start()
    for n, copy in enumerate(copies):
        copy.wait()
        for head in range(QUADS):
            out_ref[head, n * ROWS : (n + 1) * ROWS] = buf[n, :, head * HD : (head + 1) * HD]


def pack(queries, keys, values):
    return pl.pallas_call(
        pack_kernel,
        out_shape=jax.ShapeDtypeStruct((QUADS, 3 * ROWS, HD), bf16),
        in_specs=[pl.BlockSpec(memory_space=pl.ANY)] * 3,
        out_specs=vmem_spec(),
        scratch_shapes=[
            pltpu.VMEM((3,) + queries.shape, bf16),
            pltpu.SemaphoreType.DMA((3,)),
        ],
        compiler_params=pltpu.CompilerParams(vmem_limit_bytes=60 * 1024 * 1024),
        cost_estimate=pl.CostEstimate(flops=0, bytes_accessed=786432, transcendentals=0),
        name="pack",
    )(queries, keys, values)


TILE = QUADS * ROWS


ACC = HD + STAT_ROWS


def attend_kernel(members, resume, final, where_ref, order_ref, q_ref, *refs):
    count = len(members)
    kv_refs, refs = refs[:count], refs[count:]
    if resume:
        acc_in, peak_in, *refs = refs
    if final:
        out_ref, k_all, vt_all, scores = refs
    else:
        acc_out, peak_out, k_all, vt_all, scores = refs
    zp, y, c = where_ref[0], where_ref[1], where_ref[2]
    scale2 = math.log2(math.e) / math.sqrt(HD)
    halves = 2 * QUADS
    lane = lax.broadcasted_iota(jnp.int32, (1, HD), 1)
    row_half = lax.broadcasted_iota(jnp.int32, (TILE, HD), 0) // HALF
    column = lax.broadcasted_iota(jnp.int32, (TILE, HD), 1)
    key_half = jnp.full((1, HD), -1, jnp.int32)
    for n, (low, other_z, other_c) in enumerate(members):
        k_all[n, :, 0:HD] = kv_refs[n][:, low : low + ROWS].reshape(TILE, HD)
        k_all[n, :, HD:] = jnp.where(column == n * halves + row_half, 1.0, 0.0).astype(bf16)
        vt_all[n, 0:HD, :] = kv_refs[n][:, low + ROWS : low + 2 * ROWS].reshape(TILE, HD).T
        vt_all[n, HD:, :] = jnp.ones((ACC - HD, TILE), bf16)
        kz = 1 - zp if other_z else zp
        kc = 1 - c if other_c else c
        for quad in range(QUADS):
            dev = kz * 32 + quad * 8 + y * 2 + kc
            for half in range(2):
                spot = n * halves + quad * 2 + half
                key_half = jnp.where(lane == spot, order_ref[2 * dev + half], key_half)
    below = lax.broadcasted_iota(jnp.int32, (ROWS, ROWS), 0)
    right = lax.broadcasted_iota(jnp.int32, (ROWS, ROWS), 1)
    later = (below > right) & (below // HALF == right // HALF)

    for qy in range(YS):
        bias = []
        for quad in range(QUADS):
            dev = zp * 32 + quad * 8 + qy * 2 + c
            for half in range(2):
                row = jnp.where(key_half > order_ref[2 * dev + half], neg_fill, 0.0)
                bias.append(jnp.broadcast_to(row, (HALF, HD)))
        bias = jnp.concatenate(bias, axis=0).astype(bf16)
        q_blk = jnp.concatenate([q_ref[qy].reshape(TILE, HD), bias], axis=1)
        for n in range(count):
            scores[qy, n] = lax.dot_general(
                k_all[n], q_blk, (((1,), (1,)), ((), ())), preferred_element_type=f32
            )
        if not resume:
            own_later = later & (qy == y)
            for quad in range(QUADS):
                spot = slice(quad * ROWS, (quad + 1) * ROWS)
                scores[qy, 0, spot, spot] = jnp.where(own_later, neg_fill, scores[qy, 0, spot, spot])

        old = peak_in[qy, 0:1, :] if resume else jnp.full((1, TILE), neg_fill, f32)
        peak = old
        for n in range(count):
            peak = jnp.maximum(peak, jnp.max(scores[qy, n], axis=0, keepdims=True))
        acc = acc_in[qy] * jnp.exp2((old - peak) * scale2) if resume else jnp.zeros((ACC, TILE), f32)
        for n in range(count):
            p = jnp.exp2((scores[qy, n] - peak) * scale2).astype(bf16)
            acc = acc + jnp.dot(vt_all[n], p, preferred_element_type=f32)
        if not final:
            acc_out[qy] = acc
            peak_out[qy] = jnp.broadcast_to(peak, (8, TILE))
            continue
        out_ref[qy, 0:HD, :] = acc[0:HD].astype(bf16)
        rows = []
        for stat in (peak, acc[HD : HD + 1]):
            rest = stat
            for _ in range(3):
                part = rest.astype(bf16).astype(f32)
                rows.append(part)
                rest = rest - part
        rows.append(jnp.zeros((STAT_ROWS - 6, TILE), f32))
        out_ref[qy, HD:ACC, :] = jnp.concatenate(rows, axis=0).astype(bf16)


def attend(where, order, q_all, kv_blocks, members, state=(), final=False):
    def kernel(*refs):
        attend_kernel(members, len(state) > 0, final, *refs)

    if final:
        shape = jax.ShapeDtypeStruct((YS, ACC, TILE), bf16)
        specs = vmem_spec()
    else:
        shape = (
            jax.ShapeDtypeStruct((YS, ACC, TILE), f32),
            jax.ShapeDtypeStruct((YS, 8, TILE), f32),
        )
        specs = (vmem_spec(), vmem_spec())
    count = len(members)
    return pl.pallas_call(
        kernel,
        out_shape=shape,
        in_specs=[smem_spec(), smem_spec()] + [vmem_spec()] * (1 + count + len(state)),
        out_specs=specs,
        scratch_shapes=[
            pltpu.VMEM((count, TILE, 2 * HD), bf16),
            pltpu.VMEM((count, ACC, TILE), bf16),
            pltpu.VMEM((YS, count, TILE, TILE), f32),
        ],
        compiler_params=params(),
        cost_estimate=pl.CostEstimate(
            flops=count * 2048 * 2048 * 128,
            bytes_accessed=2 << 20,
            transcendentals=count << 20,
        ),
        name="attend_last" if final else "attend_more" if state else "attend_first",
    )(where, order, q_all, *kv_blocks, *state)


def merge_kernel(part_ref, out_ref):
    scale2 = math.log2(math.e) / math.sqrt(HD)
    peaks, totals = [], []
    for n in range(YS):
        stats = part_ref[n, HD : HD + STAT_ROWS, :].astype(f32)
        peaks.append((stats[0:1] + stats[1:2]) + stats[2:3])
        totals.append((stats[3:4] + stats[4:5]) + stats[5:6])
    peak = jnp.maximum(jnp.maximum(peaks[0], peaks[1]), jnp.maximum(peaks[2], peaks[3]))
    factors = [jnp.exp2((one - peak) * scale2) for one in peaks]
    total = sum(f * t for f, t in zip(factors, totals))
    inverse = 1.0 / total
    acc = jnp.zeros((HD, TILE), f32)
    for n in range(YS):
        acc = acc + part_ref[n, 0:HD, :].astype(f32) * (factors[n] * inverse)
    for quad in range(QUADS):
        out_ref[quad] = acc[:, quad * ROWS : (quad + 1) * ROWS].T.astype(bf16)


def merge(parts):
    return pl.pallas_call(
        merge_kernel,
        out_shape=jax.ShapeDtypeStruct((QUADS, ROWS, HD), bf16),
        in_specs=[vmem_spec()],
        out_specs=vmem_spec(),
        compiler_params=params(),
        cost_estimate=pl.CostEstimate(flops=1 << 20, bytes_accessed=720896, transcendentals=4096),
        name="merge",
    )(parts)


def unpack_kernel(x_ref, out_ref):
    for head in range(QUADS):
        out_ref[:, head * HD : (head + 1) * HD] = x_ref[head]


def unpack(blocks):
    return pl.pallas_call(
        unpack_kernel,
        out_shape=jax.ShapeDtypeStruct((ROWS, QUADS * HD), bf16),
        in_specs=[vmem_spec()],
        out_specs=vmem_spec(),
        compiler_params=params(),
        cost_estimate=pl.CostEstimate(flops=0, bytes_accessed=262144, transcendentals=0),
        name="unpack",
    )(blocks)


EXT = 16 + 2 * ROWS


def hyena_kernel(
    rank_ref, far_ref, near_ref, own_ref, table_ref, short_ref, long_ref,
    mixed_ref, squares_ref, hot, feats_a, feats_b, prod, base, sq,
):
    step = pl.program_id(0)
    rank = rank_ref[0]
    vocab = table_ref.shape[1]

    @pl.when(step == 0)
    def _():
        lane = lax.broadcasted_iota(jnp.int32, (128, 128), 1)

        def column(ref, valid):
            ids = jnp.where(valid, ref[...], -1)
            return jnp.broadcast_to(ids, (128, 128)).T

        for ref, valid, low, at, count in (
            (far_ref, rank >= 2, 112, 0, 16),
            (near_ref, rank >= 1, 0, 16, 128),
            (own_ref, rank >= 0, 0, 144, 128),
        ):
            col = column(ref, valid)[low : low + count]
            for v in range(vocab // 128):
                hit = col == lane[low : low + count] + v * 128
                hot[at : at + count, v * 128 : (v + 1) * 128] = jnp.where(hit, 1.0, 0.0).astype(bf16)
        sq[...] = jnp.zeros_like(sq)
        tap = lax.broadcasted_iota(jnp.int32, (TAPS, 2 * ROWS), 0)
        spot = lax.broadcasted_iota(jnp.int32, (TAPS, 2 * ROWS), 1)
        flip = jnp.where(tap + spot == TAPS, 1.0, 0.0).astype(bf16)
        base[...] = jnp.dot(long_ref[...], flip, preferred_element_type=f32)

    feats_a[...] = jnp.dot(hot[...], table_ref[1], preferred_element_type=f32)
    feats_b[...] = jnp.dot(hot[...], table_ref[3], preferred_element_type=f32)

    def short_mix(ref, stream, low, count, lanes):
        running = jnp.zeros((count, 128), f32)
        for k in range(SHORT):
            running = running + short_ref[stream, k : k + 1, lanes] * ref[low - k : low - k + count, lanes]
        return running

    for lb in range(CHAN_BLOCK // 128):
        lanes = slice(lb * 128, (lb + 1) * 128)
        for low in (16, 144):
            one = short_mix(feats_a, 0, low, 128, lanes)
            three = short_mix(feats_b, 2, low, 128, lanes)
            prod[low - 16 : low + 112, lanes] = (one * three).astype(bf16)
    feats_a[128:, :] = jnp.dot(hot[128:, :], table_ref[2], preferred_element_type=f32)
    feats_b[144:, :] = jnp.dot(hot[144:, :], table_ref[0], preferred_element_type=f32)
    chan = lax.broadcasted_iota(jnp.int32, (ROWS, CHAN_BLOCK), 1) // GSIZE
    groups_here = CHAN_BLOCK // GSIZE
    window = base[pl.ds(pl.multiple_of(step * groups_here, groups_here), groups_here)]
    conv = jnp.zeros((ROWS, CHAN_BLOCK), f32)
    for g in range(groups_here):
        row = jnp.broadcast_to(window[g : g + 1], (ROWS, 2 * ROWS))
        lags = pltpu.roll(row, 0, 1, stride=1, stride_axis=0).astype(bf16)
        every = jnp.dot(lags, prod[...], preferred_element_type=f32)
        conv = jnp.where(chan == g, every, conv)
    for lb in range(CHAN_BLOCK // 128):
        lanes = slice(lb * 128, (lb + 1) * 128)
        acc = conv[:, lanes]
        two = short_mix(feats_a, 1, 144, ROWS, lanes)
        mixed = feats_b[144:, lanes] + two * acc
        mixed_ref[:, lanes] = mixed
        sq[...] += mixed * mixed

    @pl.when(step == pl.num_programs(0) - 1)
    def _():
        squares_ref[...] = jnp.sum(sq[...].T, axis=0, keepdims=True)


def hyena(rank, far, near, own, table, short_filter, long_filter):
    streams, vocab, channels = table.shape
    return pl.pallas_call(
        hyena_kernel,
        grid=(channels // CHAN_BLOCK,),
        out_shape=(
            jax.ShapeDtypeStruct((ROWS, channels), f32),
            jax.ShapeDtypeStruct((1, ROWS), f32),
        ),
        in_specs=[
            smem_spec(),
            pl.BlockSpec((1, ROWS), lambda i: (0, 0)),
            pl.BlockSpec((1, ROWS), lambda i: (0, 0)),
            pl.BlockSpec((1, ROWS), lambda i: (0, 0)),
            pl.BlockSpec((streams, vocab, CHAN_BLOCK), lambda i: (0, 0, i)),
            pl.BlockSpec((3, SHORT, CHAN_BLOCK), lambda i: (0, 0, i)),
            pl.BlockSpec(long_filter.shape, lambda i: (0, 0)),
        ],
        out_specs=(
            pl.BlockSpec((ROWS, CHAN_BLOCK), lambda i: (0, i)),
            pl.BlockSpec((1, ROWS), lambda i: (0, 0)),
        ),
        scratch_shapes=[
            pltpu.VMEM((EXT, vocab), bf16),
            pltpu.VMEM((EXT, CHAN_BLOCK), f32),
            pltpu.VMEM((EXT, CHAN_BLOCK), f32),
            pltpu.VMEM((2 * ROWS, CHAN_BLOCK), bf16),
            pltpu.VMEM((long_filter.shape[0], 2 * ROWS), f32),
            pltpu.VMEM((ROWS, 128), f32),
        ],
        compiler_params=pltpu.CompilerParams(
            vmem_limit_bytes=60 * 1024 * 1024, dimension_semantics=("arbitrary",)
        ),
        cost_estimate=pl.CostEstimate(flops=1 << 30, bytes_accessed=5 << 20, transcendentals=0),
        name="hyena",
    )(rank, far, near, own, table, short_filter, long_filter)


def norm_kernel(channels, mixed_ref, squares_ref, gain_ref, out_ref):
    mean = squares_ref[...] / channels
    inverse = jnp.broadcast_to(lax.rsqrt(mean + eps_norm), (ROWS, ROWS)).T
    for lb in range(mixed_ref.shape[1] // 128):
        lanes = slice(lb * 128, (lb + 1) * 128)
        out_ref[:, lanes] = (mixed_ref[:, lanes] * gain_ref[:, lanes] * inverse).astype(bf16)


def norm(mixed, squares, gain, channels):
    def kernel(*refs):
        norm_kernel(channels, *refs)

    return pl.pallas_call(
        kernel,
        out_shape=jax.ShapeDtypeStruct(mixed.shape, bf16),
        in_specs=[vmem_spec()] * 3,
        out_specs=vmem_spec(),
        compiler_params=params(),
        cost_estimate=pl.CostEstimate(flops=1 << 18, bytes_accessed=800000, transcendentals=128),
        name="norm",
    )(mixed, squares, gain)


def across(squares, stride):
    groups = lax.axis_size("g")
    if stride >= groups:
        return squares
    return squares + lax.ppermute(squares, "g", [(i ^ stride, i) for i in range(groups)])


def everything(
    queries, keys, values, block_order, token_ids, stream_table, short_filter, long_filter, norm_gain
):
    groups = lax.axis_size("g")
    zp, y, c = lax.axis_index("zp"), lax.axis_index("y"), lax.axis_index("c")
    rank = ((zp * QUADS + lax.axis_index("zq")) * YS + y) * 2 + c
    devices = QUADS * 2 * YS * 2

    near = lax.ppermute(token_ids, CTX, [(i, i + 1) for i in range(devices - 1)])
    far = lax.ppermute(token_ids, CTX, [(i, i + 2) for i in range(devices - 2)])
    packed = pack(queries, keys, values)
    packed, near, far = lax.optimization_barrier((packed, near, far))
    own = lax.all_to_all(packed, "zq", 0, 0)

    mixed, squares = hyena(
        rank.reshape(1), far[None], near[None], token_ids[None],
        stream_table, short_filter, long_filter,
    )
    squares = across(squares, 2)
    own, mixed, squares = lax.optimization_barrier((own, mixed, squares))

    swap = [(0, 1), (1, 0)]
    kv_own = own[:, ROWS:]
    kv_z = lax.ppermute(kv_own, "zp", swap)
    q_all = jnp.broadcast_to(own[None, :, 0:ROWS], (YS, QUADS, ROWS, HD))
    q_all = lax.all_to_all(q_all, "y", 0, 0)
    kv_c = lax.ppermute(kv_own, "c", swap)
    squares = across(squares, 1)
    where = jnp.stack([zp, y, c])
    near_members = ((ROWS, False, False), (0, False, True))
    state = attend(where, block_order, q_all, [own, kv_c], near_members)
    kv_z, state = lax.optimization_barrier((kv_z, state))
    kv_zc = lax.ppermute(kv_z, "c", swap)
    state = attend(where, block_order, q_all, [kv_z], ((0, True, False),), state)
    parts = attend(where, block_order, q_all, [kv_zc], ((0, True, True),), state, True)
    parts, squares = lax.optimization_barrier((parts, squares))
    merged = merge(lax.all_to_all(parts, "y", 0, 0))
    merged, squares = lax.optimization_barrier((merged, across(squares, 4)))
    blocks = lax.all_to_all(merged, "zq", 0, 0)
    hyena_out = norm(mixed, squares, norm_gain[None], stream_table.shape[2] * groups)
    blocks, hyena_out = lax.optimization_barrier((blocks, hyena_out))
    return (unpack(blocks), hyena_out)


def solution(mesh):
    groups = mesh.shape["grp"]
    fine = Mesh(mesh.devices.reshape(2, QUADS, YS, 2, groups), CTX + ("g",))
    placed = (
        P(CTX, "g"),
        P(CTX, "g"),
        P(CTX, "g"),
        P(),
        P(CTX),
        P(None, None, "g"),
        P(None, None, "g"),
        P("g", None),
        P("g"),
    )
    return jax.shard_map(
        everything,
        mesh=fine,
        in_specs=placed,
        out_specs=(P(CTX, "g"), P(CTX, "g")),
        check_vma=False,
    )
```

```python
import math

import jax
import jax.numpy as jnp
from jax import lax
from jax.experimental import pallas as pl
from jax.experimental.pallas import tpu as pltpu
from jax.sharding import Mesh, PartitionSpec as P


HD = 128
ROWS = 128
HALF = 64
QUADS = 4
YS = 4
SHORT = 7
TAPS = 128
GSIZE = 16
CHAN_BLOCK = 256
STAT_ROWS = 16

neg_fill = -1e30
eps_norm = 1e-06

f32 = jnp.float32
bf16 = jnp.bfloat16
CTX = ("zp", "zq", "y", "c")
GRP = ("x", "zh")


def vmem_spec():
    return pl.BlockSpec(memory_space=pltpu.VMEM)


def smem_spec():
    return pl.BlockSpec(memory_space=pltpu.SMEM)


def params(**kw):
    return pltpu.CompilerParams(vmem_limit_bytes=48 * 1024 * 1024, **kw)


def pack_kernel(q_hbm, k_hbm, v_hbm, out_hbm, buf, out, sems, out_sems):
    loads = []
    for n, ref in enumerate((q_hbm, k_hbm, v_hbm)):
        loads.append(pltpu.make_async_copy(ref, buf.at[n], sems.at[n]))
        loads[-1].start()
    stores = []
    for n in range(3):
        loads[n].wait()
        rows = slice(n * ROWS, (n + 1) * ROWS)
        for head in range(QUADS):
            out[n, head] = buf[n, :, head * HD : (head + 1) * HD]
        stores.append(pltpu.make_async_copy(out.at[n], out_hbm.at[:, rows], out_sems.at[n]))
        stores[-1].start()
    for store in stores:
        store.wait()


def pack(queries, keys, values):
    return pl.pallas_call(
        pack_kernel,
        out_shape=jax.ShapeDtypeStruct((QUADS, 3 * ROWS, HD), bf16),
        in_specs=[pl.BlockSpec(memory_space=pl.ANY)] * 3,
        out_specs=pl.BlockSpec(memory_space=pl.ANY),
        scratch_shapes=[
            pltpu.VMEM((3,) + queries.shape, bf16),
            pltpu.VMEM((3, QUADS, ROWS, HD), bf16),
            pltpu.SemaphoreType.DMA((3,)),
            pltpu.SemaphoreType.DMA((3,)),
        ],
        compiler_params=pltpu.CompilerParams(vmem_limit_bytes=60 * 1024 * 1024),
        cost_estimate=pl.CostEstimate(flops=0, bytes_accessed=786432, transcendentals=0),
        name="pack",
    )(queries, keys, values)


TILE = QUADS * ROWS


ACC = HD + STAT_ROWS


def attend_kernel(members, resume, final, where_ref, order_ref, q_ref, *refs):
    count = len(members)
    kv_refs, refs = refs[:count], refs[count:]
    if resume:
        acc_in, peak_in, *refs = refs
    if final:
        out_hbm, k_all, vt_all, scores, out_ref, out_sems = refs
        stores = []
    else:
        acc_out, peak_out, k_all, vt_all, scores = refs
    zp, y, c = where_ref[0], where_ref[1], where_ref[2]
    scale2 = math.log2(math.e) / math.sqrt(HD)
    halves = 2 * QUADS
    lane = lax.broadcasted_iota(jnp.int32, (1, HD), 1)
    row_half = lax.broadcasted_iota(jnp.int32, (TILE, HD), 0) // HALF
    column = lax.broadcasted_iota(jnp.int32, (TILE, HD), 1)
    key_half = jnp.full((1, HD), -1, jnp.int32)
    for n, (low, other_z, other_c) in enumerate(members):
        k_all[n, :, 0:HD] = kv_refs[n][:, low : low + ROWS].reshape(TILE, HD)
        k_all[n, :, HD:] = jnp.where(column == n * halves + row_half, 1.0, 0.0).astype(bf16)
        vt_all[n, 0:HD, :] = kv_refs[n][:, low + ROWS : low + 2 * ROWS].reshape(TILE, HD).T
        vt_all[n, HD:, :] = jnp.ones((ACC - HD, TILE), bf16)
        kz = 1 - zp if other_z else zp
        kc = 1 - c if other_c else c
        for quad in range(QUADS):
            dev = kz * 32 + quad * 8 + y * 2 + kc
            for half in range(2):
                spot = n * halves + quad * 2 + half
                key_half = jnp.where(lane == spot, order_ref[2 * dev + half], key_half)
    below = lax.broadcasted_iota(jnp.int32, (ROWS, ROWS), 0)
    right = lax.broadcasted_iota(jnp.int32, (ROWS, ROWS), 1)
    later = (below > right) & (below // HALF == right // HALF)

    for qy in range(YS):
        bias = []
        for quad in range(QUADS):
            dev = zp * 32 + quad * 8 + qy * 2 + c
            for half in range(2):
                row = jnp.where(key_half > order_ref[2 * dev + half], neg_fill, 0.0)
                bias.append(jnp.broadcast_to(row, (HALF, HD)))
        bias = jnp.concatenate(bias, axis=0).astype(bf16)
        q_blk = jnp.concatenate([q_ref[qy].reshape(TILE, HD), bias], axis=1)
        for n in range(count):
            scores[qy, n] = lax.dot_general(
                k_all[n], q_blk, (((1,), (1,)), ((), ())), preferred_element_type=f32
            )
        if not resume:
            own_later = later & (qy == y)
            for quad in range(QUADS):
                spot = slice(quad * ROWS, (quad + 1) * ROWS)
                scores[qy, 0, spot, spot] = jnp.where(own_later, neg_fill, scores[qy, 0, spot, spot])

        old = peak_in[qy, 0:1, :] if resume else jnp.full((1, TILE), neg_fill, f32)
        peak = old
        for n in range(count):
            peak = jnp.maximum(peak, jnp.max(scores[qy, n], axis=0, keepdims=True))
        acc = acc_in[qy] * jnp.exp2((old - peak) * scale2) if resume else jnp.zeros((ACC, TILE), f32)
        for n in range(count):
            p = jnp.exp2((scores[qy, n] - peak) * scale2).astype(bf16)
            acc = acc + jnp.dot(vt_all[n], p, preferred_element_type=f32)
        if not final:
            acc_out[qy] = acc
            peak_out[qy] = jnp.broadcast_to(peak, (8, TILE))
            continue
        out_ref[qy, 0:HD, :] = acc[0:HD].astype(bf16)
        rows = []
        for stat in (peak, acc[HD : HD + 1]):
            rest = stat
            for _ in range(3):
                part = rest.astype(bf16).astype(f32)
                rows.append(part)
                rest = rest - part
        rows.append(jnp.zeros((STAT_ROWS - 6, TILE), f32))
        out_ref[qy, HD:ACC, :] = jnp.concatenate(rows, axis=0).astype(bf16)
        stores.append(pltpu.make_async_copy(out_ref.at[qy], out_hbm.at[qy], out_sems.at[qy]))
        stores[-1].start()
    if final:
        for store in stores:
            store.wait()


def attend(where, order, q_all, kv_blocks, members, state=(), final=False):
    def kernel(*refs):
        attend_kernel(members, len(state) > 0, final, *refs)

    if final:
        shape = jax.ShapeDtypeStruct((YS, ACC, TILE), bf16)
        specs = pl.BlockSpec(memory_space=pl.ANY)
        extra = [pltpu.VMEM((YS, ACC, TILE), bf16), pltpu.SemaphoreType.DMA((YS,))]
    else:
        shape = (
            jax.ShapeDtypeStruct((YS, ACC, TILE), f32),
            jax.ShapeDtypeStruct((YS, 8, TILE), f32),
        )
        specs = (vmem_spec(), vmem_spec())
        extra = []
    count = len(members)
    return pl.pallas_call(
        kernel,
        out_shape=shape,
        in_specs=[smem_spec(), smem_spec()] + [vmem_spec()] * (1 + count + len(state)),
        out_specs=specs,
        scratch_shapes=[
            pltpu.VMEM((count, TILE, 2 * HD), bf16),
            pltpu.VMEM((count, ACC, TILE), bf16),
            pltpu.VMEM((YS, count, TILE, TILE), f32),
        ]
        + extra,
        compiler_params=params(),
        cost_estimate=pl.CostEstimate(
            flops=count * 2048 * 2048 * 128,
            bytes_accessed=2 << 20,
            transcendentals=count << 20,
        ),
        name="attend_last" if final else "attend_more" if state else "attend_first",
    )(where, order, q_all, *kv_blocks, *state)


def merge_kernel(part_ref, out_ref):
    scale2 = math.log2(math.e) / math.sqrt(HD)
    peaks, totals = [], []
    for n in range(YS):
        stats = part_ref[n, HD : HD + STAT_ROWS, :].astype(f32)
        peaks.append((stats[0:1] + stats[1:2]) + stats[2:3])
        totals.append((stats[3:4] + stats[4:5]) + stats[5:6])
    peak = jnp.maximum(jnp.maximum(peaks[0], peaks[1]), jnp.maximum(peaks[2], peaks[3]))
    factors = [jnp.exp2((one - peak) * scale2) for one in peaks]
    total = sum(f * t for f, t in zip(factors, totals))
    inverse = 1.0 / total
    acc = jnp.zeros((HD, TILE), f32)
    for n in range(YS):
        acc = acc + part_ref[n, 0:HD, :].astype(f32) * (factors[n] * inverse)
    for quad in range(QUADS):
        out_ref[quad] = acc[:, quad * ROWS : (quad + 1) * ROWS].T.astype(bf16)


def merge(parts):
    return pl.pallas_call(
        merge_kernel,
        out_shape=jax.ShapeDtypeStruct((QUADS, ROWS, HD), bf16),
        in_specs=[vmem_spec()],
        out_specs=vmem_spec(),
        compiler_params=params(),
        cost_estimate=pl.CostEstimate(flops=1 << 20, bytes_accessed=720896, transcendentals=4096),
        name="merge",
    )(parts)


def unpack_kernel(x_ref, out_ref):
    for head in range(QUADS):
        out_ref[:, head * HD : (head + 1) * HD] = x_ref[head]


def unpack(blocks):
    return pl.pallas_call(
        unpack_kernel,
        out_shape=jax.ShapeDtypeStruct((ROWS, QUADS * HD), bf16),
        in_specs=[vmem_spec()],
        out_specs=vmem_spec(),
        compiler_params=params(),
        cost_estimate=pl.CostEstimate(flops=0, bytes_accessed=262144, transcendentals=0),
        name="unpack",
    )(blocks)


EXT = 16 + 2 * ROWS


def hyena_kernel(
    rank_ref, far_ref, near_ref, own_ref, table_ref, short_ref, long_ref,
    mixed_ref, squares_ref, hot, feats_a, feats_b, prod, base, sq,
):
    step = pl.program_id(0)
    rank = rank_ref[0]
    vocab = table_ref.shape[1]

    @pl.when(step == 0)
    def _():
        lane = lax.broadcasted_iota(jnp.int32, (128, 128), 1)

        def column(ref, valid):
            ids = jnp.where(valid, ref[...], -1)
            return jnp.broadcast_to(ids, (128, 128)).T

        for ref, valid, low, at, count in (
            (far_ref, rank >= 2, 112, 0, 16),
            (near_ref, rank >= 1, 0, 16, 128),
            (own_ref, rank >= 0, 0, 144, 128),
        ):
            col = column(ref, valid)[low : low + count]
            for v in range(vocab // 128):
                hit = col == lane[low : low + count] + v * 128
                hot[at : at + count, v * 128 : (v + 1) * 128] = jnp.where(hit, 1.0, 0.0).astype(bf16)
        sq[...] = jnp.zeros_like(sq)
        tap = lax.broadcasted_iota(jnp.int32, (TAPS, 2 * ROWS), 0)
        spot = lax.broadcasted_iota(jnp.int32, (TAPS, 2 * ROWS), 1)
        flip = jnp.where(tap + spot == TAPS, 1.0, 0.0).astype(bf16)
        base[...] = jnp.dot(long_ref[...], flip, preferred_element_type=f32)

    feats_a[...] = jnp.dot(hot[...], table_ref[1], preferred_element_type=f32)
    feats_b[...] = jnp.dot(hot[...], table_ref[3], preferred_element_type=f32)

    def short_mix(ref, stream, low, count, lanes):
        running = jnp.zeros((count, 128), f32)
        for k in range(SHORT):
            running = running + short_ref[stream, k : k + 1, lanes] * ref[low - k : low - k + count, lanes]
        return running

    for lb in range(CHAN_BLOCK // 128):
        lanes = slice(lb * 128, (lb + 1) * 128)
        for low in (16, 144):
            one = short_mix(feats_a, 0, low, 128, lanes)
            three = short_mix(feats_b, 2, low, 128, lanes)
            prod[low - 16 : low + 112, lanes] = (one * three).astype(bf16)
    feats_a[128:, :] = jnp.dot(hot[128:, :], table_ref[2], preferred_element_type=f32)
    feats_b[144:, :] = jnp.dot(hot[144:, :], table_ref[0], preferred_element_type=f32)
    chan = lax.broadcasted_iota(jnp.int32, (ROWS, CHAN_BLOCK), 1) // GSIZE
    groups_here = CHAN_BLOCK // GSIZE
    window = base[pl.ds(pl.multiple_of(step * groups_here, groups_here), groups_here)]
    conv = jnp.zeros((ROWS, CHAN_BLOCK), f32)
    for g in range(groups_here):
        row = jnp.broadcast_to(window[g : g + 1], (ROWS, 2 * ROWS))
        lags = pltpu.roll(row, 0, 1, stride=1, stride_axis=0).astype(bf16)
        every = jnp.dot(lags, prod[...], preferred_element_type=f32)
        conv = jnp.where(chan == g, every, conv)
    for lb in range(CHAN_BLOCK // 128):
        lanes = slice(lb * 128, (lb + 1) * 128)
        acc = conv[:, lanes]
        two = short_mix(feats_a, 1, 144, ROWS, lanes)
        mixed = feats_b[144:, lanes] + two * acc
        mixed_ref[:, lanes] = mixed
        sq[...] += mixed * mixed

    @pl.when(step == pl.num_programs(0) - 1)
    def _():
        squares_ref[...] = jnp.sum(sq[...].T, axis=0, keepdims=True)


def hyena(rank, far, near, own, table, short_filter, long_filter):
    streams, vocab, channels = table.shape
    return pl.pallas_call(
        hyena_kernel,
        grid=(channels // CHAN_BLOCK,),
        out_shape=(
            jax.ShapeDtypeStruct((ROWS, channels), f32),
            jax.ShapeDtypeStruct((1, ROWS), f32),
        ),
        in_specs=[
            smem_spec(),
            pl.BlockSpec((1, ROWS), lambda i: (0, 0)),
            pl.BlockSpec((1, ROWS), lambda i: (0, 0)),
            pl.BlockSpec((1, ROWS), lambda i: (0, 0)),
            pl.BlockSpec((streams, vocab, CHAN_BLOCK), lambda i: (0, 0, i)),
            pl.BlockSpec((3, SHORT, CHAN_BLOCK), lambda i: (0, 0, i)),
            pl.BlockSpec(long_filter.shape, lambda i: (0, 0)),
        ],
        out_specs=(
            pl.BlockSpec((ROWS, CHAN_BLOCK), lambda i: (0, i)),
            pl.BlockSpec((1, ROWS), lambda i: (0, 0)),
        ),
        scratch_shapes=[
            pltpu.VMEM((EXT, vocab), bf16),
            pltpu.VMEM((EXT, CHAN_BLOCK), f32),
            pltpu.VMEM((EXT, CHAN_BLOCK), f32),
            pltpu.VMEM((2 * ROWS, CHAN_BLOCK), bf16),
            pltpu.VMEM((long_filter.shape[0], 2 * ROWS), f32),
            pltpu.VMEM((ROWS, 128), f32),
        ],
        compiler_params=pltpu.CompilerParams(
            vmem_limit_bytes=60 * 1024 * 1024, dimension_semantics=("arbitrary",)
        ),
        cost_estimate=pl.CostEstimate(flops=1 << 30, bytes_accessed=5 << 20, transcendentals=0),
        name="hyena",
    )(rank, far, near, own, table, short_filter, long_filter)


def norm_kernel(channels, mixed_ref, squares_ref, other_ref, gain_ref, out_ref):
    mean = (squares_ref[...] + other_ref[...]) / channels
    inverse = jnp.broadcast_to(lax.rsqrt(mean + eps_norm), (ROWS, ROWS)).T
    for lb in range(mixed_ref.shape[1] // 128):
        lanes = slice(lb * 128, (lb + 1) * 128)
        out_ref[:, lanes] = (mixed_ref[:, lanes] * gain_ref[:, lanes] * inverse).astype(bf16)


def norm(mixed, squares, other, gain, channels):
    def kernel(*refs):
        norm_kernel(channels, *refs)

    return pl.pallas_call(
        kernel,
        out_shape=jax.ShapeDtypeStruct(mixed.shape, bf16),
        in_specs=[vmem_spec()] * 4,
        out_specs=vmem_spec(),
        compiler_params=params(),
        cost_estimate=pl.CostEstimate(flops=1 << 18, bytes_accessed=800000, transcendentals=128),
        name="norm",
    )(mixed, squares, other, gain)


def across(squares, stride):
    members = lax.axis_size("x")
    if stride >= members:
        return jnp.zeros_like(squares)
    return lax.ppermute(squares, "x", [(i ^ stride, i) for i in range(members)])


def everything(
    queries, keys, values, block_order, token_ids, stream_table, short_filter, long_filter, norm_gain
):
    groups = lax.axis_size(("x", "zh"))
    zp, y, c = lax.axis_index("zp"), lax.axis_index("y"), lax.axis_index("c")
    rank = ((zp * QUADS + lax.axis_index("zq")) * YS + y) * 2 + c
    devices = QUADS * 2 * YS * 2

    near = lax.ppermute(token_ids, CTX, [(i, i + 1) for i in range(devices - 1)])
    far = lax.ppermute(token_ids, CTX, [(i, i + 2) for i in range(devices - 2)])
    packed = pack(queries, keys, values)
    own = lax.all_to_all(packed, "zq", 0, 0)

    mixed, squares = hyena(
        rank.reshape(1), far[None], near[None], token_ids[None],
        stream_table, short_filter, long_filter,
    )
    own, mixed, squares = lax.optimization_barrier((own, mixed, squares))

    swap = [(0, 1), (1, 0)]
    kv_own = own[:, ROWS:]
    kv_z = lax.ppermute(kv_own, "zp", swap)
    q_all = jnp.broadcast_to(own[None, :, 0:ROWS], (YS, QUADS, ROWS, HD))
    q_all = lax.all_to_all(q_all, "y", 0, 0)
    kv_c = lax.ppermute(kv_own, "c", swap)
    where = jnp.stack([zp, y, c])
    other = lax.ppermute(squares, "zh", swap)
    near_members = ((ROWS, False, False), (0, False, True))
    state = attend(where, block_order, q_all, [own, kv_c], near_members)
    kv_z, state = lax.optimization_barrier((kv_z, state))
    kv_zc = lax.ppermute(kv_z, "c", swap)
    state = attend(where, block_order, q_all, [kv_z], ((0, True, False),), state)
    parts = attend(where, block_order, q_all, [kv_zc], ((0, True, True),), state, True)
    parts, squares, other = lax.optimization_barrier((parts, squares, other))
    merged = lax.all_to_all(parts, "y", 0, 0)
    squares = squares + other
    squares = squares + across(squares, 2)
    merged, squares = lax.optimization_barrier((merged, squares))
    merged = merge(merged)
    blocks = lax.all_to_all(merged, "zq", 0, 0)
    other = across(squares, 1)
    hyena_out = norm(mixed, squares, other, norm_gain[None], stream_table.shape[2] * groups)
    blocks, hyena_out = lax.optimization_barrier((blocks, hyena_out))
    return (unpack(blocks), hyena_out)


def solution(mesh):
    groups = mesh.shape["grp"]
    fine = Mesh(mesh.devices.reshape(2, QUADS, YS, 2, groups // 2, 2), CTX + GRP)
    placed = (
        P(CTX, GRP),
        P(CTX, GRP),
        P(CTX, GRP),
        P(),
        P(CTX),
        P(None, None, GRP),
        P(None, None, GRP),
        P(GRP, None),
        P(GRP),
    )
    return jax.shard_map(
        everything,
        mesh=fine,
        in_specs=placed,
        out_specs=(P(CTX, GRP), P(CTX, GRP)),
        check_vma=False,
    )
```

```python
import math

import jax
import jax.numpy as jnp
from jax import lax
from jax.experimental import pallas as pl
from jax.experimental.pallas import tpu as pltpu
from jax.sharding import Mesh, PartitionSpec as P


HD = 128
ROWS = 128
HALF = 64
QUADS = 4
YS = 4
SHORT = 7
TAPS = 128
GSIZE = 16
CHAN_BLOCK = 256
STAT_ROWS = 16

neg_fill = -1e30
eps_norm = 1e-06

f32 = jnp.float32
bf16 = jnp.bfloat16
CTX = ("zp", "zq", "y", "c")
GRP = ("x", "zh")


def vmem_spec():
    return pl.BlockSpec(memory_space=pltpu.VMEM)


def smem_spec():
    return pl.BlockSpec(memory_space=pltpu.SMEM)


def params(**kw):
    return pltpu.CompilerParams(vmem_limit_bytes=48 * 1024 * 1024, **kw)


def pack_kernel(q_hbm, k_hbm, v_hbm, out_hbm, buf, out, sems, out_sems):
    loads = []
    for n, ref in enumerate((q_hbm, k_hbm, v_hbm)):
        loads.append(pltpu.make_async_copy(ref, buf.at[n], sems.at[n]))
        loads[-1].start()
    stores = []
    for n in range(3):
        loads[n].wait()
        rows = slice(n * ROWS, (n + 1) * ROWS)
        for head in range(QUADS):
            out[n, head] = buf[n, :, head * HD : (head + 1) * HD]
        stores.append(pltpu.make_async_copy(out.at[n], out_hbm.at[:, rows], out_sems.at[n]))
        stores[-1].start()
    for store in stores:
        store.wait()


def pack(queries, keys, values):
    return pl.pallas_call(
        pack_kernel,
        out_shape=jax.ShapeDtypeStruct((QUADS, 3 * ROWS, HD), bf16),
        in_specs=[pl.BlockSpec(memory_space=pl.ANY)] * 3,
        out_specs=pl.BlockSpec(memory_space=pl.ANY),
        scratch_shapes=[
            pltpu.VMEM((3,) + queries.shape, bf16),
            pltpu.VMEM((3, QUADS, ROWS, HD), bf16),
            pltpu.SemaphoreType.DMA((3,)),
            pltpu.SemaphoreType.DMA((3,)),
        ],
        compiler_params=pltpu.CompilerParams(vmem_limit_bytes=60 * 1024 * 1024),
        cost_estimate=pl.CostEstimate(flops=0, bytes_accessed=786432, transcendentals=0),
        name="pack",
    )(queries, keys, values)


TILE = QUADS * ROWS


HALVES = 2 * QUADS
STAGES = (
    ((ROWS, False, False), (0, False, True)),
    ((0, True, False),),
    ((0, True, True),),
)
ACC = HD + STAT_ROWS


def attend_kernel(stage, resume, final, bias_ref, own_ref, q_ref, *refs):
    lows = [low for low, _, _ in STAGES[stage]]
    count = len(lows)
    kv_refs, refs = refs[:count], refs[count:]
    if resume:
        acc_in, peak_in, *refs = refs
    if final:
        out_hbm, k_all, vt_all, scores, out_ref, out_sems = refs
        stores = []
    else:
        acc_out, peak_out, k_all, vt_all, scores = refs
    scale2 = math.log2(math.e) / math.sqrt(HD)
    row_half = lax.broadcasted_iota(jnp.int32, (TILE, HD), 0) // HALF
    column = lax.broadcasted_iota(jnp.int32, (TILE, HD), 1)
    for n, low in enumerate(lows):
        k_all[n, :, 0:HD] = kv_refs[n][:, low : low + ROWS].reshape(TILE, HD)
        k_all[n, :, HD:] = jnp.where(column == n * HALVES + row_half, 1.0, 0.0).astype(bf16)
        vt_all[n, 0:HD, :] = kv_refs[n][:, low + ROWS : low + 2 * ROWS].reshape(TILE, HD).T
        vt_all[n, HD:, :] = jnp.ones((ACC - HD, TILE), bf16)
    below = lax.broadcasted_iota(jnp.int32, (ROWS, ROWS), 0)
    right = lax.broadcasted_iota(jnp.int32, (ROWS, ROWS), 1)
    later = (below > right) & (below // HALF == right // HALF)

    for qy in range(YS):
        bias = jnp.concatenate(
            [
                jnp.broadcast_to(bias_ref[stage, row : row + 1], (HALF, HD))
                for row in range(qy * HALVES, (qy + 1) * HALVES)
            ],
            axis=0,
        ).astype(bf16)
        q_blk = jnp.concatenate([q_ref[qy].reshape(TILE, HD), bias], axis=1)
        for n in range(count):
            scores[qy, n] = lax.dot_general(
                k_all[n], q_blk, (((1,), (1,)), ((), ())), preferred_element_type=f32
            )
        if not resume:
            own_later = later & (own_ref[qy : qy + 1] > 0.5)
            for quad in range(QUADS):
                spot = slice(quad * ROWS, (quad + 1) * ROWS)
                scores[qy, 0, spot, spot] = jnp.where(own_later, neg_fill, scores[qy, 0, spot, spot])

        old = peak_in[qy, 0:1, :] if resume else jnp.full((1, TILE), neg_fill, f32)
        peak = old
        for n in range(count):
            peak = jnp.maximum(peak, jnp.max(scores[qy, n], axis=0, keepdims=True))
        acc = acc_in[qy] * jnp.exp2((old - peak) * scale2) if resume else jnp.zeros((ACC, TILE), f32)
        for n in range(count):
            p = jnp.exp2((scores[qy, n] - peak) * scale2).astype(bf16)
            acc = acc + jnp.dot(vt_all[n], p, preferred_element_type=f32)
        if not final:
            acc_out[qy] = acc
            peak_out[qy] = jnp.broadcast_to(peak, (8, TILE))
            continue
        out_ref[qy, 0:HD, :] = acc[0:HD].astype(bf16)
        rows = []
        for stat in (peak, acc[HD : HD + 1]):
            rest = stat
            for _ in range(3):
                part = rest.astype(bf16).astype(f32)
                rows.append(part)
                rest = rest - part
        rows.append(jnp.zeros((STAT_ROWS - 6, TILE), f32))
        out_ref[qy, HD:ACC, :] = jnp.concatenate(rows, axis=0).astype(bf16)
        stores.append(pltpu.make_async_copy(out_ref.at[qy], out_hbm.at[qy], out_sems.at[qy]))
        stores[-1].start()
    if final:
        for store in stores:
            store.wait()


def attend(stage, bias, own, q_all, kv_blocks, state=(), final=False):
    def kernel(*refs):
        attend_kernel(stage, len(state) > 0, final, *refs)

    if final:
        shape = jax.ShapeDtypeStruct((YS, ACC, TILE), bf16)
        specs = pl.BlockSpec(memory_space=pl.ANY)
        extra = [pltpu.VMEM((YS, ACC, TILE), bf16), pltpu.SemaphoreType.DMA((YS,))]
    else:
        shape = (
            jax.ShapeDtypeStruct((YS, ACC, TILE), f32),
            jax.ShapeDtypeStruct((YS, 8, TILE), f32),
        )
        specs = (vmem_spec(), vmem_spec())
        extra = []
    count = len(STAGES[stage])
    return pl.pallas_call(
        kernel,
        out_shape=shape,
        in_specs=[vmem_spec()] * (3 + count + len(state)),
        out_specs=specs,
        scratch_shapes=[
            pltpu.VMEM((count, TILE, 2 * HD), bf16),
            pltpu.VMEM((count, ACC, TILE), bf16),
            pltpu.VMEM((YS, count, TILE, TILE), f32),
        ]
        + extra,
        compiler_params=params(),
        cost_estimate=pl.CostEstimate(
            flops=count * 2048 * 2048 * 128,
            bytes_accessed=2 << 20,
            transcendentals=count << 20,
        ),
        name="attend_last" if final else "attend_more" if state else "attend_first",
    )(bias, own, q_all, *kv_blocks, *state)


def merge_kernel(part_ref, out_ref):
    scale2 = math.log2(math.e) / math.sqrt(HD)
    peaks, totals = [], []
    for n in range(YS):
        stats = part_ref[n, HD : HD + STAT_ROWS, :].astype(f32)
        peaks.append((stats[0:1] + stats[1:2]) + stats[2:3])
        totals.append((stats[3:4] + stats[4:5]) + stats[5:6])
    peak = jnp.maximum(jnp.maximum(peaks[0], peaks[1]), jnp.maximum(peaks[2], peaks[3]))
    factors = [jnp.exp2((one - peak) * scale2) for one in peaks]
    total = sum(f * t for f, t in zip(factors, totals))
    inverse = 1.0 / total
    acc = jnp.zeros((HD, TILE), f32)
    for n in range(YS):
        acc = acc + part_ref[n, 0:HD, :].astype(f32) * (factors[n] * inverse)
    for quad in range(QUADS):
        out_ref[quad] = acc[:, quad * ROWS : (quad + 1) * ROWS].T.astype(bf16)


def merge(parts):
    return pl.pallas_call(
        merge_kernel,
        out_shape=jax.ShapeDtypeStruct((QUADS, ROWS, HD), bf16),
        in_specs=[vmem_spec()],
        out_specs=vmem_spec(),
        compiler_params=params(),
        cost_estimate=pl.CostEstimate(flops=1 << 20, bytes_accessed=720896, transcendentals=4096),
        name="merge",
    )(parts)


def unpack_kernel(x_ref, out_ref):
    for head in range(QUADS):
        out_ref[:, head * HD : (head + 1) * HD] = x_ref[head]


def unpack(blocks):
    return pl.pallas_call(
        unpack_kernel,
        out_shape=jax.ShapeDtypeStruct((ROWS, QUADS * HD), bf16),
        in_specs=[vmem_spec()],
        out_specs=vmem_spec(),
        compiler_params=params(),
        cost_estimate=pl.CostEstimate(flops=0, bytes_accessed=262144, transcendentals=0),
        name="unpack",
    )(blocks)


EXT = 16 + 2 * ROWS


def attention_bias(place_ref, order_ref, bias_ref, flag_ref):
    zp, y, c = place_ref[1], place_ref[2], place_ref[3]
    lane = lax.broadcasted_iota(jnp.int32, (1, HD), 1)
    for stage, members in enumerate(STAGES):
        key_half = jnp.full((1, HD), -1, jnp.int32)
        for n, (_, other_z, other_c) in enumerate(members):
            kz = 1 - zp if other_z else zp
            kc = 1 - c if other_c else c
            for half in range(HALVES):
                dev = kz * 32 + (half // 2) * 8 + y * 2 + kc
                key_half = jnp.where(
                    lane == n * HALVES + half, order_ref[2 * dev + half % 2], key_half
                )
        for qy in range(YS):
            rows = []
            for half in range(HALVES):
                dev = zp * 32 + (half // 2) * 8 + qy * 2 + c
                rows.append(jnp.where(key_half > order_ref[2 * dev + half % 2], neg_fill, 0.0))
            bias_ref[stage, qy * HALVES : (qy + 1) * HALVES, :] = jnp.concatenate(rows, axis=0)
    row = lax.broadcasted_iota(jnp.int32, flag_ref.shape, 0)
    flag_ref[...] = jnp.where(row == y, 1.0, 0.0)


def hyena_kernel(
    place_ref, order_ref, far_ref, near_ref, own_ref, table_ref, short_ref, long_ref,
    mixed_ref, squares_ref, bias_ref, flag_ref, hot, feats_a, feats_b, prod, base, sq,
):
    step = pl.program_id(0)
    rank = place_ref[0]
    vocab = table_ref.shape[1]

    @pl.when(step == 0)
    def _():
        lane = lax.broadcasted_iota(jnp.int32, (128, 128), 1)

        def column(ref, valid):
            ids = jnp.where(valid, ref[...], -1)
            return jnp.broadcast_to(ids, (128, 128)).T

        for ref, valid, low, at, count in (
            (far_ref, rank >= 2, 112, 0, 16),
            (near_ref, rank >= 1, 0, 16, 128),
            (own_ref, rank >= 0, 0, 144, 128),
        ):
            col = column(ref, valid)[low : low + count]
            for v in range(vocab // 128):
                hit = col == lane[low : low + count] + v * 128
                hot[at : at + count, v * 128 : (v + 1) * 128] = jnp.where(hit, 1.0, 0.0).astype(bf16)
        sq[...] = jnp.zeros_like(sq)
        attention_bias(place_ref, order_ref, bias_ref, flag_ref)
        tap = lax.broadcasted_iota(jnp.int32, (TAPS, 2 * ROWS), 0)
        spot = lax.broadcasted_iota(jnp.int32, (TAPS, 2 * ROWS), 1)
        flip = jnp.where(tap + spot == TAPS, 1.0, 0.0).astype(bf16)
        base[...] = jnp.dot(long_ref[...], flip, preferred_element_type=f32)

    feats_a[...] = jnp.dot(hot[...], table_ref[1], preferred_element_type=f32)
    feats_b[...] = jnp.dot(hot[...], table_ref[3], preferred_element_type=f32)

    def short_mix(ref, stream, low, count, lanes):
        running = jnp.zeros((count, 128), f32)
        for k in range(SHORT):
            running = running + short_ref[stream, k : k + 1, lanes] * ref[low - k : low - k + count, lanes]
        return running

    for lb in range(CHAN_BLOCK // 128):
        lanes = slice(lb * 128, (lb + 1) * 128)
        for low in (16, 144):
            one = short_mix(feats_a, 0, low, 128, lanes)
            three = short_mix(feats_b, 2, low, 128, lanes)
            prod[low - 16 : low + 112, lanes] = (one * three).astype(bf16)
    feats_a[128:, :] = jnp.dot(hot[128:, :], table_ref[2], preferred_element_type=f32)
    feats_b[144:, :] = jnp.dot(hot[144:, :], table_ref[0], preferred_element_type=f32)
    chan = lax.broadcasted_iota(jnp.int32, (ROWS, CHAN_BLOCK), 1) // GSIZE
    groups_here = CHAN_BLOCK // GSIZE
    window = base[pl.ds(pl.multiple_of(step * groups_here, groups_here), groups_here)]
    conv = jnp.zeros((ROWS, CHAN_BLOCK), f32)
    for g in range(groups_here):
        row = jnp.broadcast_to(window[g : g + 1], (ROWS, 2 * ROWS))
        lags = pltpu.roll(row, 0, 1, stride=1, stride_axis=0).astype(bf16)
        every = jnp.dot(lags, prod[...], preferred_element_type=f32)
        conv = jnp.where(chan == g, every, conv)
    for lb in range(CHAN_BLOCK // 128):
        lanes = slice(lb * 128, (lb + 1) * 128)
        acc = conv[:, lanes]
        two = short_mix(feats_a, 1, 144, ROWS, lanes)
        mixed = feats_b[144:, lanes] + two * acc
        mixed_ref[:, lanes] = mixed
        sq[...] += mixed * mixed

    @pl.when(step == pl.num_programs(0) - 1)
    def _():
        squares_ref[...] = jnp.sum(sq[...].T, axis=0, keepdims=True)


def hyena(place, order, far, near, own, table, short_filter, long_filter):
    streams, vocab, channels = table.shape
    return pl.pallas_call(
        hyena_kernel,
        grid=(channels // CHAN_BLOCK,),
        out_shape=(
            jax.ShapeDtypeStruct((ROWS, channels), f32),
            jax.ShapeDtypeStruct((1, ROWS), f32),
            jax.ShapeDtypeStruct((len(STAGES), YS * HALVES, HD), f32),
            jax.ShapeDtypeStruct((8, HD), f32),
        ),
        in_specs=[
            smem_spec(),
            smem_spec(),
            pl.BlockSpec((1, ROWS), lambda i: (0, 0)),
            pl.BlockSpec((1, ROWS), lambda i: (0, 0)),
            pl.BlockSpec((1, ROWS), lambda i: (0, 0)),
            pl.BlockSpec((streams, vocab, CHAN_BLOCK), lambda i: (0, 0, i)),
            pl.BlockSpec((3, SHORT, CHAN_BLOCK), lambda i: (0, 0, i)),
            pl.BlockSpec(long_filter.shape, lambda i: (0, 0)),
        ],
        out_specs=(
            pl.BlockSpec((ROWS, CHAN_BLOCK), lambda i: (0, i)),
            pl.BlockSpec((1, ROWS), lambda i: (0, 0)),
            pl.BlockSpec((len(STAGES), YS * HALVES, HD), lambda i: (0, 0, 0)),
            pl.BlockSpec((8, HD), lambda i: (0, 0)),
        ),
        scratch_shapes=[
            pltpu.VMEM((EXT, vocab), bf16),
            pltpu.VMEM((EXT, CHAN_BLOCK), f32),
            pltpu.VMEM((EXT, CHAN_BLOCK), f32),
            pltpu.VMEM((2 * ROWS, CHAN_BLOCK), bf16),
            pltpu.VMEM((long_filter.shape[0], 2 * ROWS), f32),
            pltpu.VMEM((ROWS, 128), f32),
        ],
        compiler_params=pltpu.CompilerParams(
            vmem_limit_bytes=60 * 1024 * 1024, dimension_semantics=("arbitrary",)
        ),
        cost_estimate=pl.CostEstimate(flops=1 << 30, bytes_accessed=5 << 20, transcendentals=0),
        name="hyena",
    )(place, order, far, near, own, table, short_filter, long_filter)


def norm_kernel(channels, mixed_ref, a, b, c, d, gain_ref, out_ref):
    mean = ((a[...] + b[...]) + (c[...] + d[...])) / channels
    inverse = jnp.broadcast_to(lax.rsqrt(mean + eps_norm), (ROWS, ROWS)).T
    for lb in range(mixed_ref.shape[1] // 128):
        lanes = slice(lb * 128, (lb + 1) * 128)
        out_ref[:, lanes] = (mixed_ref[:, lanes] * gain_ref[:, lanes] * inverse).astype(bf16)


def norm(mixed, sums, gain, channels):
    def kernel(*refs):
        norm_kernel(channels, *refs)

    return pl.pallas_call(
        kernel,
        out_shape=jax.ShapeDtypeStruct(mixed.shape, bf16),
        in_specs=[vmem_spec()] * 6,
        out_specs=vmem_spec(),
        compiler_params=params(),
        cost_estimate=pl.CostEstimate(flops=1 << 18, bytes_accessed=800000, transcendentals=128),
        name="norm",
    )(mixed, *sums, gain)


def across(squares, mask):
    members = lax.axis_size("x")
    if mask >= members:
        return jnp.zeros_like(squares)
    return lax.ppermute(squares, "x", [(i ^ mask, i) for i in range(members)])


def everything(
    queries, keys, values, block_order, token_ids, stream_table, short_filter, long_filter, norm_gain
):
    groups = lax.axis_size(("x", "zh"))
    zp, y, c = lax.axis_index("zp"), lax.axis_index("y"), lax.axis_index("c")
    rank = ((zp * QUADS + lax.axis_index("zq")) * YS + y) * 2 + c
    devices = QUADS * 2 * YS * 2

    near = lax.ppermute(token_ids, CTX, [(i, i + 1) for i in range(devices - 1)])
    far = lax.ppermute(token_ids, CTX, [(i, i + 2) for i in range(devices - 2)])
    packed = pack(queries, keys, values)
    own = lax.all_to_all(packed, "zq", 0, 0)

    mixed, squares, bias, flags = hyena(
        jnp.stack([rank, zp, y, c]), block_order, far[None], near[None], token_ids[None],
        stream_table, short_filter, long_filter,
    )
    own, mixed, squares, bias, flags = lax.optimization_barrier((own, mixed, squares, bias, flags))

    swap = [(0, 1), (1, 0)]
    kv_own = own[:, ROWS:]
    kv_z = lax.ppermute(kv_own, "zp", swap)
    q_all = jnp.broadcast_to(own[None, :, 0:ROWS], (YS, QUADS, ROWS, HD))
    q_all = lax.all_to_all(q_all, "y", 0, 0)
    kv_c = lax.ppermute(kv_own, "c", swap)
    other = lax.ppermute(squares, "zh", swap)
    state = attend(0, bias, flags, q_all, [own, kv_c])
    kv_z, state = lax.optimization_barrier((kv_z, state))
    kv_zc = lax.ppermute(kv_z, "c", swap)
    state = attend(1, bias, flags, q_all, [kv_z], state)
    parts = attend(2, bias, flags, q_all, [kv_zc], state, True)
    parts, squares, other = lax.optimization_barrier((parts, squares, other))
    merged = lax.all_to_all(parts, "y", 0, 0)
    squares = squares + other
    sums = [squares]
    for mask in (1, 3, 2):
        sums.append(across(squares, mask))
    merged = merge(merged)
    blocks = lax.all_to_all(merged, "zq", 0, 0)
    hyena_out = norm(mixed, sums, norm_gain[None], stream_table.shape[2] * groups)
    blocks, hyena_out = lax.optimization_barrier((blocks, hyena_out))
    return (unpack(blocks), hyena_out)


def solution(mesh):
    groups = mesh.shape["grp"]
    fine = Mesh(mesh.devices.reshape(2, QUADS, YS, 2, groups // 2, 2), CTX + GRP)
    placed = (
        P(CTX, GRP),
        P(CTX, GRP),
        P(CTX, GRP),
        P(),
        P(CTX),
        P(None, None, GRP),
        P(None, None, GRP),
        P(GRP, None),
        P(GRP),
    )
    return jax.shard_map(
        everything,
        mesh=fine,
        in_specs=placed,
        out_specs=(P(CTX, GRP), P(CTX, GRP)),
        check_vma=False,
    )
```
